128 devices in a mesh: ctx: 16 (over y, z), head: 8 (over x, core).
Axes of the slice: x: 4, y: 4, z: 4, core: 2. Of those that a mesh axis runs over, the one named last changes fastest.
Arguments:
- queries: bfloat16 [16384, 64, 128], P('ctx', 'head'), may hold values from -8 to 8
- key_rows: bfloat16 [16384, 64, 128], P('ctx', 'head'), may hold values from -4 to 4
- value_rows: bfloat16 [16384, 64, 128], P('ctx', 'head'), may hold values from -12 to 12
- grad_normed: bfloat16 [16384, 64, 128], P('ctx', 'head'), may hold values from -6 to 6
- norm_gain: float32 [64, 128], P('head'), may hold values from 0.1 to 1.9
- document_starts: int32 [6], replicated, may hold values from 0 to 16256, as said below
Outputs:
- normed: bfloat16 [16384, 64, 128], P('ctx', 'head')
- grad_queries: bfloat16 [16384, 64, 128], P('ctx', 'head')
- grad_keys: bfloat16 [16384, 64, 128], P('ctx', 'head')
- grad_values: bfloat16 [16384, 64, 128], P('ctx', 'head')
- grad_gain: float32 [64, 128], P('head')
The draws below stay inside these ranges and needn't reach their ends.
Inputs may be any that keep to these rules, and one draw needn't show every extreme that they name: `document_starts`: strictly increasing multiples of 128; the first is 0 and the last is 16256.
All inputs are finite; a program needn't handle non-finite values.
Results may differ from the reference program's by a relative error of at most 0.0057.
Values sent between devices are 32-bit elements; how exact they have to be, the bound alone decides.
A program may use at most 128 MiB of HBM per device.

```python
import math
import jax
import jax.numpy as jnp
from jax import lax

HEADS = 64
HEAD_DIM = 128
TILE = 512
ALIGN = 128
DOCS = 6
TOKENS = 16384


def rough_entries(entry_key, shape):
    return jax.random.normal(entry_key, shape, jnp.float32)


def draw_queries(key, part):
    entry_key, row_key = jax.random.split(jax.random.fold_in(key, 11), 2)
    entries = rough_entries(entry_key, (TOKENS, HEADS, HEAD_DIM))
    row_scale = jnp.exp(jax.random.uniform(row_key, (TOKENS, 1, 1), jnp.float32, 0.0, math.log(10.0)))
    return jnp.clip(entries * row_scale * HEAD_DIM ** (-0.25), -8.0, 8.0).astype(jnp.bfloat16)


def draw_value_rows(key, part):
    entry_key, row_key, jitter_key = jax.random.split(jax.random.fold_in(key, 23), 3)
    entries = rough_entries(entry_key, (TOKENS, HEADS, HEAD_DIM))
    spread = math.log(3.0)
    head_steps = jnp.arange(HEADS, dtype=jnp.float32) / (HEADS - 1)
    jitter = jax.random.uniform(jitter_key, (HEADS,), jnp.float32, -0.3, 0.3)
    head_scale = jnp.exp(spread * head_steps + jitter)[None, :, None]
    row_scale = jnp.exp(jax.random.uniform(row_key, (TOKENS, 1, 1), jnp.float32, 0.0, math.log(3.0)))
    return jnp.clip(entries * head_scale * row_scale, -12.0, 12.0).astype(jnp.bfloat16)


def draw_grad_normed(key, part):
    entry_key, row_key = jax.random.split(jax.random.fold_in(key, 37), 2)
    entries = rough_entries(entry_key, (TOKENS, HEADS, HEAD_DIM))
    row_scale = jnp.exp(jax.random.uniform(row_key, (TOKENS, 1, 1), jnp.float32, 0.0, math.log(3.0)))
    rising = jnp.exp(math.log(3.0) * jnp.arange(TOKENS, dtype=jnp.float32) / (TOKENS - 1))[:, None, None]
    return jnp.clip(0.3 * entries * row_scale * rising, -6.0, 6.0).astype(jnp.bfloat16)


def draw_document_starts(key, part):
    block_count = TOKENS // ALIGN
    shuffled = jax.random.permutation(jax.random.fold_in(key, 41), block_count - 2) + 1
    inner = jnp.sort(shuffled[:DOCS - 2])
    first_block = jnp.zeros((1,), jnp.int32)
    final_block = jnp.full((1,), block_count - 1, jnp.int32)
    return (jnp.concatenate([first_block, inner.astype(jnp.int32), final_block]) * ALIGN).astype(jnp.int32)


def shard_levels(own_key, dims, shards, smallest, largest):
    factor_of = 1.0
    for axis_at, blocks in shards:
        heights = jax.random.uniform(jax.random.fold_in(jax.random.fold_in(own_key, 6), axis_at), (blocks,), jnp.float32, smallest / len(shards), largest / len(shards))
        factor_of = factor_of * jnp.repeat(jnp.exp(heights), dims[axis_at] // blocks).reshape((-1,) + (1,) * (len(dims) - 1 - axis_at))
    return factor_of


def gaussian(stream_key, extent, scale, bound, shards=(), kind=jnp.bfloat16):
    values = scale * jax.random.normal(stream_key, extent, jnp.float32)
    if shards:
        values = values * shard_levels(stream_key, extent, shards, -0.22, 0.18)
    return jnp.clip(values, -bound, bound).astype(kind)


def setup_inputs(seed: int = 0) -> dict:
    streams_of = jax.random.split(jax.random.key(seed), 7)
    queries = draw_queries(jax.random.fold_in(streams_of[6], 71), 0)
    key_rows = gaussian(streams_of[1], (TOKENS, HEADS, HEAD_DIM), (HEAD_DIM ** -0.25), 4.0, ((0, 16), (1, 8)))
    value_rows = draw_value_rows(jax.random.fold_in(streams_of[6], 71), 0)
    grad_normed = draw_grad_normed(jax.random.fold_in(streams_of[6], 71), 0)
    norm_gain = jnp.clip(1.0 + 0.18 * jax.random.normal(streams_of[4], (HEADS, HEAD_DIM), jnp.float32), 0.1, 1.9)
    document_starts = draw_document_starts(jax.random.fold_in(streams_of[6], 71), 0)
    return {"queries": queries, "key_rows": key_rows, "value_rows": value_rows, "grad_normed": grad_normed, "norm_gain": norm_gain, "document_starts": document_starts}


EPSILON = 1e-06

def token_documents(starts, positions):
    return lax.optimization_barrier(jnp.sum((starts[None, :] <= positions[:, None]).astype(jnp.int32), axis=1)).astype(jnp.int32) - 1

def rounded(array):
    return lax.optimization_barrier(array.astype(jnp.bfloat16)).astype(jnp.float32)

def reference(queries, key_rows, value_rows, grad_normed, norm_gain, document_starts):
    tile_count = TOKENS // TILE
    feature_count = HEADS * HEAD_DIM
    positions = jnp.arange(TOKENS, dtype=jnp.int32)
    documents = token_documents(document_starts, positions).reshape(tile_count, TILE)
    prior_docs = token_documents(document_starts, jnp.arange(tile_count, dtype=jnp.int32) * TILE - 1)
    last_docs = documents[:, -1]
    causal = jnp.arange(TILE)[:, None] >= jnp.arange(TILE)[None, :]

    def shaped(array):
        return array.reshape(tile_count, TILE, HEADS, HEAD_DIM)

    def tile_masks(tile_docs, prior_doc, last_doc):
        entering = (tile_docs == prior_doc).astype(jnp.float32)
        leaving = (tile_docs == last_doc).astype(jnp.float32)
        within = (causal & (tile_docs[:, None] == tile_docs[None, :])).astype(jnp.float32)
        keep_flag = (last_doc == prior_doc).astype(jnp.float32)
        return (entering, leaving, within, keep_flag)

    def forward_step(carried_in, inputs):
        carried, gain_sum = carried_in
        query_tile, key_tile, value_tile, upstream_tile, tile_docs, prior_doc, last_doc = inputs
        entering, leaving, within, keep_flag = tile_masks(tile_docs, prior_doc, last_doc)
        query_f = query_tile.astype(jnp.float32)
        key_f = key_tile.astype(jnp.float32)
        value_f = value_tile.astype(jnp.float32)
        attention = rounded(jnp.einsum('thd,shd->hts', query_f, key_f) * within[None])
        state_bf = rounded(carried)
        intra_out = jnp.einsum('hts,shd->thd', attention, value_f)
        inter_out = jnp.einsum('thd,hde->the', query_f, state_bf)
        attended = intra_out + entering[:, None, None] * inter_out
        squares = lax.optimization_barrier(jnp.sum(attended * attended, axis=(1, 2)))
        inverse = 1.0 / jnp.sqrt(squares / feature_count + EPSILON)
        scaled = attended * inverse[:, None, None]
        normed = (scaled * norm_gain).astype(jnp.bfloat16)
        upstream = upstream_tile.astype(jnp.float32)
        weighted = upstream * norm_gain
        cross_sum = lax.optimization_barrier(jnp.sum(weighted * attended, axis=(1, 2)))
        grad_att = rounded(inverse[:, None, None] * weighted - attended * (inverse ** 3 * cross_sum / feature_count)[:, None, None])
        grad_scores = rounded(jnp.einsum('the,she->hts', grad_att, value_f) * within[None])
        query_intra = jnp.einsum('hts,shd->thd', grad_scores, key_f)
        query_inter = jnp.einsum('the,hde->thd', grad_att, state_bf)
        grad_query = (query_intra + entering[:, None, None] * query_inter).astype(jnp.bfloat16)
        tile_state = jnp.einsum('thd,the->hde', key_f * leaving[:, None, None], value_f)
        next_state = tile_state + keep_flag * carried
        gain_sum = gain_sum + lax.optimization_barrier(jnp.sum(upstream * scaled, axis=0))
        return ((next_state, gain_sum), (normed, grad_att.astype(jnp.bfloat16), grad_query))
    inputs = (shaped(queries), shaped(key_rows), shaped(value_rows), shaped(grad_normed), documents, prior_docs, last_docs)
    start_state = jnp.zeros((HEADS, HEAD_DIM, HEAD_DIM), jnp.float32)
    start_gain = jnp.zeros((HEADS, HEAD_DIM), jnp.float32)
    (final_state, gain_sum), (normed, grad_att, grad_queries) = lax.scan(forward_step, (start_state, start_gain), inputs)

    def backward_step(exit_state, inputs_back):
        query_tile, key_tile, value_tile, grad_tile, tile_docs, prior_doc, last_doc = inputs_back
        entering, leaving, within, keep_flag = tile_masks(tile_docs, prior_doc, last_doc)
        query_f = query_tile.astype(jnp.float32)
        key_f = key_tile.astype(jnp.float32)
        value_f = value_tile.astype(jnp.float32)
        grad_f = grad_tile.astype(jnp.float32)
        attention = rounded(jnp.einsum('thd,shd->hts', query_f, key_f) * within[None])
        grad_scores = rounded(jnp.einsum('the,she->hts', grad_f, value_f) * within[None])
        exit_bf = rounded(exit_state)
        key_intra = jnp.einsum('hts,thd->shd', grad_scores, query_f)
        key_inter = jnp.einsum('she,hde->shd', value_f, exit_bf)
        value_intra = jnp.einsum('hts,the->she', attention, grad_f)
        value_inter = jnp.einsum('shd,hde->she', key_f, exit_bf)
        grad_key = (key_intra + leaving[:, None, None] * key_inter).astype(jnp.bfloat16)
        grad_value = (value_intra + leaving[:, None, None] * value_inter).astype(jnp.bfloat16)
        tile_grad = jnp.einsum('thd,the->hde', query_f * entering[:, None, None], grad_f)
        earlier_state = tile_grad + keep_flag * exit_state
        return (earlier_state, (grad_key, grad_value))
    inputs_back = (shaped(queries), shaped(key_rows), shaped(value_rows), grad_att, documents, prior_docs, last_docs)
    first_grad, (grad_keys, grad_values) = lax.scan(backward_step, start_state, inputs_back, reverse=True)
    whole = (TOKENS, HEADS, HEAD_DIM)
    grad_gain = gain_sum / math.sqrt(TOKENS)
    return (normed.reshape(whole), grad_queries.reshape(whole), grad_keys.reshape(whole), grad_values.reshape(whole), grad_gain)
```

```python
import functools
import math

import jax
import jax.numpy as jnp
from jax import lax
from jax.experimental import pallas as pl
from jax.experimental.pallas import tpu as pltpu
from jax.sharding import PartitionSpec as P

HEADS = 64
HEAD_DIM = 128
EPSILON = 1e-06
TOKENS = 16384
SHARDS = 16
PEERS = 8
ROWS = 1024
LOCAL = 8
B = 128
TILES = ROWS // B
GROUPS = 2
G = LOCAL // GROUPS
PIECE = HEAD_DIM // SHARDS
MESH = pl.DeviceIdType.MESH
F32 = jnp.float32
BF16 = jnp.bfloat16

OFFSETS = sorted(
    range(1, SHARDS), key=lambda o: -(min(o // 4, 4 - o // 4) + min(o % 4, 4 - o % 4))
)


def nn(a, b):
    return lax.dot_general(a, b, (((1,), (0,)), ((), ())), preferred_element_type=F32)


def nt(a, b):
    return lax.dot_general(a, b, (((1,), (1,)), ((), ())), preferred_element_type=F32)


def tn(a, b):
    return lax.dot_general(a, b, (((0,), (0,)), ((), ())), preferred_element_type=F32)


def loop(count, body):
    def step(i, carry):
        body(i)
        return carry

    lax.fori_loop(0, count, step, 0)


def kernel(
    q_hbm, k_hbm, v_hbm, u_hbm, gain_ref, starts_ref,
    n_out, dq_out, dk_out, dv_out, dgain_ref,
    q_raw, k_raw, v_raw, u_raw,
    qh, kh, vh, uh, gh, ah, ath, bth, tmp, att, lbuf, rbuf,
    sqa, cra, invb, cob, gpart,
    st, rx, px, inc, st2, rx2, px2, inc2,
    stat_rx, stat_tx, gain_rx, gain_tx,
    kc_sm, mp_sm, nz_sm, keep_sm,
    in_sem, out_sem, s1, r1, s2, r2, s3, r3, s4, r4, hs, hr, gs, gr_sem,
):
    me = lax.axis_index("ctx")
    my_head = lax.axis_index("head")
    y, z = me // 4, lax.rem(me, 4)

    def at_offset(o):
        return lax.rem(y + o // 4, 4) * 4 + lax.rem(z + o % 4, 4)

    hbm_in = (k_hbm, v_hbm, q_hbm, u_hbm)
    raw_in = (k_raw, v_raw, q_raw, u_raw)

    def load(a, c):
        rows = pl.ds(c * B, B)
        return pltpu.make_async_copy(hbm_in[a].at[rows], raw_in[a].at[rows], in_sem.at[a, c])

    for c in range(TILES):
        load(0, c).start()
        load(1, c).start()
    for c in range(TILES):
        load(2, c).start()
        load(3, c).start()

    barrier = pltpu.get_barrier_semaphore()
    for k in range(1, SHARDS):
        pl.semaphore_signal(
            barrier, inc=1, device_id={"ctx": lax.rem(me + k, SHARDS)}, device_id_type=MESH
        )
    for k in range(1, PEERS):
        pl.semaphore_signal(
            barrier, inc=1, device_id={"head": lax.rem(my_head + k, PEERS)}, device_id_type=MESH
        )

    docs = starts_ref.shape[0]

    def opens(position, width):
        found = jnp.int32(0)
        for d in range(docs):
            found = found + (starts_ref[d] // width == position).astype(jnp.int32)
        return 1.0 - jnp.minimum(found, 1).astype(F32)

    running = jnp.float32(1.0)
    for c in range(TILES):
        flag = opens(me * TILES + c, B)
        running = running * flag
        kc_sm[c] = flag
        mp_sm[c] = running
    running = jnp.float32(1.0)
    for c in reversed(range(TILES)):
        nz_sm[c] = running
        running = running * kc_sm[c]

    def shard_flag(i):
        keep_sm[i] = opens(i, ROWS)

    loop(SHARDS, shard_flag)

    row = lax.broadcasted_iota(jnp.int32, (B, B), 0)
    col = lax.broadcasted_iota(jnp.int32, (B, B), 1)

    def lower(x):
        return jnp.where(row >= col, x, 0.0).astype(BF16)

    def upper(x):
        return jnp.where(row <= col, x, 0.0).astype(BF16)

    def unpack(raw, out, c):
        out[:, c] = jnp.swapaxes(raw[pl.ds(pl.multiple_of(c * B, B), B)], 0, 1)

    def states(g):
        heads = range(g * G, (g + 1) * G)

        def body(c):
            flag = kc_sm[c]
            for h in heads:
                part = tn(kh[h, c], vh[h, c])
                kept = flag * st[h].reshape(B, B)
                lbuf[h, c] = kept
                st[h] = (part + kept).reshape(SHARDS, PIECE, B)

        loop(TILES, body)

    def group(g):
        return pl.ds(g * G, G)

    def scatter(src, dst, ssem, rsem, g):
        for n, o in enumerate(OFFSETS):
            p = at_offset(o)
            pltpu.make_async_remote_copy(
                src.at[group(g), p], dst.at[me, group(g)], ssem.at[g, n], rsem.at[g, me],
                device_id={"ctx": p}, device_id_type=MESH,
            ).start()
        dst[me, group(g)] = src[group(g), me]

    def scatter_done(src, dst, ssem, rsem, g):
        for n, o in enumerate(OFFSETS):
            p = at_offset(o)
            pltpu.make_async_remote_copy(
                src.at[group(g), p], dst.at[me, group(g)], ssem.at[g, n], rsem.at[g, me],
                device_id={"ctx": p}, device_id_type=MESH,
            ).wait_send()

    def back(px, inc, ssem, rsem, g, i):
        return pltpu.make_async_remote_copy(
            px.at[i, group(g)], inc.at[me, group(g)], ssem.at[g, i], rsem.at[g, me],
            device_id={"ctx": i}, device_id_type=MESH,
        )

    def chain(src, rx, px, inc, s_in, r_in, s_out, r_out, g, forward):
        first = 0 if forward else SHARDS - 1
        px[first, group(g)] = jnp.zeros((G, PIECE, B), F32)

        def step(turn, total):
            i = turn if forward else SHARDS - 1 - turn

            @pl.when(i != me)
            def _():
                pltpu.make_async_remote_copy(
                    src.at[group(g), i], rx.at[i, group(g)], s_in.at[g, 0], r_in.at[g, i],
                    device_id={"ctx": i}, device_id_type=MESH,
                ).wait_recv()

            total = rx[i, group(g)] + keep_sm[i] * total

            @pl.when(turn < SHARDS - 1)
            def _():
                px[i + 1 if forward else i - 1, group(g)] = total

            @pl.when(i != me)
            def _():
                back(px, inc, s_out, r_out, g, i).start()

            return total

        lax.fori_loop(0, SHARDS, step, jnp.zeros((G, PIECE, B), F32))
        inc[me, group(g)] = px[me, group(g)]

    def arrived(px, inc, ssem, rsem, g):
        for o in OFFSETS:
            p = at_offset(o)
            pltpu.make_async_remote_copy(
                px.at[p, group(g)], inc.at[p, group(g)], ssem.at[g, p], rsem.at[g, p],
                device_id={"ctx": p}, device_id_type=MESH,
            ).wait_recv()

    def back_done(px, inc, ssem, rsem, g):
        for o in OFFSETS:
            back(px, inc, ssem, rsem, g, at_offset(o)).wait_send()

    st[...] = jnp.zeros_like(st)

    def first_load(c):
        load(0, c).wait()
        load(1, c).wait()
        unpack(k_raw, kh, c)
        unpack(v_raw, vh, c)

    loop(TILES, first_load)
    states(0)
    pl.semaphore_wait(barrier, SHARDS - 1 + PEERS - 1)
    scatter(st, rx, s1, r1, 0)
    for g in range(1, GROUPS):
        states(g)
        scatter(st, rx, s1, r1, g)

    def second_load(c):
        load(2, c).wait()
        load(3, c).wait()
        unpack(q_raw, qh, c)
        unpack(u_raw, uh, c)

    loop(TILES, second_load)

    def scores(g):
        def body(c):
            for h in range(g * G, (g + 1) * G):
                ah[h, c] = lower(nt(qh[h, c], kh[h, c]))

        loop(TILES, body)

    def scores_t(g):
        def body(c):
            for h in range(g * G, (g + 1) * G):
                ath[h, c] = upper(nt(kh[h, c], qh[h, c]))

        loop(TILES, body)

    scores(0)
    for g in range(GROUPS):
        chain(st, rx, px, inc, s1, r1, s2, r2, g, True)
        if g + 1 < GROUPS:
            scores(g + 1)
    for g in range(GROUPS):
        scores_t(g)

    for g in range(GROUPS):
        arrived(px, inc, s2, r2, g)

        def body(c, g=g):
            sq = jnp.zeros((B, B), F32) if g == 0 else sqa[c]
            cr = jnp.zeros((B, B), F32) if g == 0 else cra[c]
            reach = mp_sm[c]
            for h in range(g * G, (g + 1) * G):
                entry = (lbuf[h, c] + reach * inc[:, h].reshape(B, B)).astype(BF16)
                rbuf[h, c] = entry
                out = nn(
                    jnp.concatenate([ah[h, c], qh[h, c]], axis=1),
                    jnp.concatenate([vh[h, c], entry], axis=0),
                )
                att[h, c] = out
                sq = sq + out * out
                cr = cr + uh[h, c].astype(F32) * gain_ref[h : h + 1, :] * out
            sqa[c] = sq
            cra[c] = cr

        loop(TILES, body)

    sq_cols = jnp.zeros((B, B), F32)
    cr_cols = jnp.zeros((B, B), F32)
    for c in range(TILES):
        sq_cols = jnp.where(col == c, jnp.sum(sqa[c], axis=1, keepdims=True), sq_cols)
        cr_cols = jnp.where(col == c, jnp.sum(cra[c], axis=1, keepdims=True), cr_cols)
    stat_tx[0] = jnp.transpose(sq_cols)[:TILES]
    stat_tx[1] = jnp.transpose(cr_cols)[:TILES]

    def tell(k):
        to = lax.rem(my_head + k, PEERS)
        return pltpu.make_async_remote_copy(
            stat_tx, stat_rx.at[my_head], hs.at[k], hr.at[my_head],
            device_id={"head": to}, device_id_type=MESH,
        )

    for k in range(1, PEERS):
        tell(k).start()
    stat_rx[my_head] = stat_tx[...]
    for k in range(1, PEERS):
        source = lax.rem(my_head + k, PEERS)
        pltpu.make_async_remote_copy(
            stat_tx, stat_rx.at[source], hs.at[k], hr.at[source],
            device_id={"head": source}, device_id_type=MESH,
        ).wait_recv()
    sums = stat_rx[0]
    for k in range(1, PEERS):
        sums = sums + stat_rx[k]
    features = HEADS * HEAD_DIM
    inverse = 1.0 / jnp.sqrt(sums[0] / features + EPSILON)
    pull = inverse * inverse * inverse * sums[1] / features
    inv_cols = jnp.transpose(jnp.concatenate([inverse] * (B // TILES), axis=0))
    pull_cols = jnp.transpose(jnp.concatenate([pull] * (B // TILES), axis=0))
    for c in range(TILES):
        invb[c] = jnp.broadcast_to(inv_cols[:, c : c + 1], (B, B))
        cob[c] = jnp.broadcast_to(pull_cols[:, c : c + 1], (B, B))

    gpart[...] = jnp.zeros_like(gpart)
    st2[...] = jnp.zeros_like(st2)
    for g in range(GROUPS):

        def body(turn, g=g):
            c = TILES - 1 - turn
            flag = kc_sm[c]
            inv = invb[c]
            co = cob[c]
            for h in range(g * G, (g + 1) * G):
                gain = gain_ref[h : h + 1, :]
                out = att[h, c]
                up = uh[h, c].astype(F32)
                scaled = out * inv
                ah[h, c] = (scaled * gain).astype(BF16)
                grad = (inv * (up * gain) - out * co).astype(BF16)
                gh[h, c] = grad
                gpart[h] += jnp.sum((up * scaled).reshape(B // 8, 8, B), axis=0)
                later = st2[h].reshape(B, B)
                lbuf[h, c] = later
                st2[h] = (flag * (tn(qh[h, c], grad) + later)).reshape(SHARDS, PIECE, B)

        loop(TILES, body)
        scatter(st2, rx2, s3, r3, g)

    for h in range(LOCAL):
        gain_tx[h : h + 1, :] = jnp.sum(gpart[h], axis=0, keepdims=True)

    def tell_gain(k):
        to = lax.rem(me + k, SHARDS)
        return pltpu.make_async_remote_copy(
            gain_tx, gain_rx.at[me], gs.at[k], gr_sem.at[me],
            device_id={"ctx": to}, device_id_type=MESH,
        )

    for k in range(1, SHARDS):
        tell_gain(k).start()
    gain_rx[me] = gain_tx[...]

    def store(stage, out, a, c):
        rows = pl.ds(c * B, B)
        return pltpu.make_async_copy(stage.at[rows], out.at[rows], out_sem.at[a, c])

    def pack(value, stage, out, a, c):
        stage[pl.ds(pl.multiple_of(c * B, B), B)] = jnp.swapaxes(value, 0, 1)
        store(stage, out, a, c).start()

    def grad_q(g):
        def body(c):
            for h in range(g * G, (g + 1) * G):
                grad = gh[h, c]
                b = lower(nt(grad, vh[h, c]))
                bth[h, c] = upper(nt(vh[h, c], grad))
                rbuf[h, c] = (nn(b, kh[h, c]) + nt(grad, rbuf[h, c])).astype(BF16)

        loop(TILES, body)

    def put_normed(c):
        pack(ah[:, c], q_raw, n_out, 0, c)

    loop(TILES, put_normed)
    for g in range(GROUPS):
        grad_q(g)
        chain(st2, rx2, px2, inc2, s3, r3, s4, r4, g, False)

    def put_dq(c):
        pack(rbuf[:, c], u_raw, dq_out, 1, c)

    loop(TILES, put_dq)

    for k in range(1, SHARDS):
        source = lax.rem(me + k, SHARDS)
        pltpu.make_async_remote_copy(
            gain_tx, gain_rx.at[source], gs.at[k], gr_sem.at[source],
            device_id={"ctx": source}, device_id_type=MESH,
        ).wait_recv()
    total = gain_rx[0]
    for k in range(1, SHARDS):
        total = total + gain_rx[k]
    dgain_ref[...] = total / math.sqrt(TOKENS)

    for g in range(GROUPS):
        arrived(px2, inc2, s4, r4, g)

        def body(c, g=g):
            reach = nz_sm[c]
            for h in range(g * G, (g + 1) * G):
                leave = (lbuf[h, c] + reach * inc2[:, h].reshape(B, B)).astype(BF16)
                dk = nn(bth[h, c], qh[h, c]) + nt(vh[h, c], leave)
                dv = nn(
                    jnp.concatenate([ath[h, c], kh[h, c]], axis=1),
                    jnp.concatenate([gh[h, c], leave], axis=0),
                )
                ah[h, c] = dk.astype(BF16)
                uh[h, c] = dv.astype(BF16)
            if g == GROUPS - 1:
                pack(ah[:, c], k_raw, dk_out, 2, c)
                pack(uh[:, c], v_raw, dv_out, 3, c)

        loop(TILES, body)

    for g in range(GROUPS):
        scatter_done(st, rx, s1, r1, g)
        back_done(px, inc, s2, r2, g)
        scatter_done(st2, rx2, s3, r3, g)
        back_done(px2, inc2, s4, r4, g)
    for k in range(1, PEERS):
        tell(k).wait_send()
    for k in range(1, SHARDS):
        tell_gain(k).wait_send()

    def drain(c):
        store(q_raw, n_out, 0, c).wait()
        store(u_raw, dq_out, 1, c).wait()
        store(k_raw, dk_out, 2, c).wait()
        store(v_raw, dv_out, 3, c).wait()

    loop(TILES, drain)


def local(queries, key_rows, value_rows, grad_normed, norm_gain, document_starts):
    anywhere = pl.BlockSpec(memory_space=pl.ANY)
    vmem = pl.BlockSpec(memory_space=pltpu.VMEM)
    tiles = (LOCAL, TILES, B, B)
    raw = pltpu.VMEM((ROWS, LOCAL, HEAD_DIM), BF16)
    narrow = pltpu.VMEM(tiles, BF16)
    wide = pltpu.VMEM(tiles, F32)
    stats = pltpu.VMEM((TILES, B, B), F32)
    state = pltpu.VMEM((LOCAL, SHARDS, PIECE, B), F32)
    pieces = pltpu.VMEM((SHARDS, LOCAL, PIECE, B), F32)
    dma = pltpu.SemaphoreType.DMA
    big = jax.ShapeDtypeStruct((ROWS, LOCAL, HEAD_DIM), BF16)
    return pl.pallas_call(
        kernel,
        out_shape=(big, big, big, big, jax.ShapeDtypeStruct((LOCAL, HEAD_DIM), F32)),
        in_specs=[anywhere] * 4 + [vmem, pl.BlockSpec(memory_space=pltpu.SMEM)],
        out_specs=(anywhere,) * 4 + (vmem,),
        scratch_shapes=[raw] * 4
        + [narrow] * 8
        + [pltpu.VMEM((8, 128), F32), wide, wide, narrow]
        + [stats] * 4
        + [pltpu.VMEM((LOCAL, 8, B), F32)]
        + [state, pieces, pieces, pieces, state, pieces, pieces, pieces]
        + [
            pltpu.VMEM((PEERS, 2, TILES, B), F32),
            pltpu.VMEM((2, TILES, B), F32),
            pltpu.VMEM((SHARDS, LOCAL, B), F32),
            pltpu.VMEM((LOCAL, B), F32),
        ]
        + [pltpu.SMEM((TILES,), F32)] * 3
        + [pltpu.SMEM((SHARDS,), F32)]
        + [dma((4, TILES)), dma((4, TILES))]
        + [dma((GROUPS, SHARDS))] * 8
        + [dma((PEERS,))] * 2
        + [dma((SHARDS,))] * 2,
        compiler_params=pltpu.CompilerParams(
            collective_id=0, has_side_effects=True, vmem_limit_bytes=67043328
        ),
    )(queries, key_rows, value_rows, grad_normed, norm_gain, document_starts)


def solution(mesh):
    rows = P("ctx", "head", None)
    return jax.shard_map(
        local,
        mesh=mesh,
        in_specs=(rows, rows, rows, rows, P("head", None), P()),
        out_specs=(rows, rows, rows, rows, P("head", None)),
        check_vma=False,
    )
```

```python
import functools
import math

import jax
import jax.numpy as jnp
from jax import lax
from jax.experimental import pallas as pl
from jax.experimental.pallas import tpu as pltpu
from jax.sharding import PartitionSpec as P

HEADS = 64
HEAD_DIM = 128
EPSILON = 1e-06
TOKENS = 16384
SHARDS = 16
PEERS = 8
ROWS = 1024
LOCAL = 8
B = 128
TILES = ROWS // B
HALF = ROWS // 2
STEP = 4
PAIR = 2
LIMIT = 32 << 20
LIMIT2 = 12 << 20
GROUPS = 2
G = LOCAL // GROUPS
PIECE = HEAD_DIM // SHARDS
MESH = pl.DeviceIdType.MESH
F32 = jnp.float32
BF16 = jnp.bfloat16

OFFSETS = sorted(
    range(1, SHARDS), key=lambda o: -(min(o // 4, 4 - o // 4) + min(o % 4, 4 - o % 4))
)


def nn(a, b):
    return lax.dot_general(a, b, (((1,), (0,)), ((), ())), preferred_element_type=F32)


def nt(a, b):
    return lax.dot_general(a, b, (((1,), (1,)), ((), ())), preferred_element_type=F32)


def tn(a, b):
    return lax.dot_general(a, b, (((0,), (0,)), ((), ())), preferred_element_type=F32)


def turn(a):
    return jnp.transpose(a)


def loop(count, body):
    def step(i, carry):
        body(i)
        return carry

    lax.fori_loop(0, count, step, 0)


def flags(starts_ref):
    def opens(position, width):
        found = jnp.int32(0)
        for d in range(starts_ref.shape[0]):
            found = found + (starts_ref[d] // width == position).astype(jnp.int32)
        return 1.0 - jnp.minimum(found, 1).astype(F32)

    return opens


def kernel(
    q_hbm, k_hbm, v_hbm, u_hbm, gain_hbm, starts_hbm,
    n_tok, dq_tok, qh, kh, vh, gh, ath, bth, lbuf, inc2, reach_ref, dgain_ref,
    gain_ref, starts_ref, q_raw, k_raw, v_raw, u_raw,
    uh, ah, att, rbuf,
    sqa, cra, invb, cob, gpart,
    st, rx, px, inc, st2, rx2, px2,
    stat_rx, stat_tx, gain_rx, gain_tx,
    kc_sm, mp_sm, keep_sm,
    small_sem, in_sem, s1, r1, s2, r2, s3, r3, s4, r4, hs, hr, gs, gr_sem,
):
    me = lax.axis_index("ctx")
    my_head = lax.axis_index("head")
    y, z = me // 4, lax.rem(me, 4)

    def at_offset(o):
        return lax.rem(y + o // 4, 4) * 4 + lax.rem(z + o % 4, 4)

    hbm_in = (k_hbm, v_hbm, q_hbm, u_hbm)
    raw_in = (k_raw, v_raw, q_raw, u_raw)

    def load(a, c):
        rows = pl.ds(c * HALF, HALF)
        return pltpu.make_async_copy(hbm_in[a].at[rows], raw_in[a].at[rows], in_sem.at[a, c])

    small = [
        pltpu.make_async_copy(starts_hbm, starts_ref, small_sem.at[0]),
        pltpu.make_async_copy(gain_hbm, gain_ref, small_sem.at[1]),
    ]
    for copy in small:
        copy.start()
    for a, b in ((0, 1), (2, 3)):
        for c in range(2):
            load(a, c).start()
            load(b, c).start()

    barrier = pltpu.get_barrier_semaphore()
    for k in range(1, SHARDS):
        pl.semaphore_signal(
            barrier, inc=1, device_id={"ctx": lax.rem(me + k, SHARDS)}, device_id_type=MESH
        )
    for k in range(1, PEERS):
        pl.semaphore_signal(
            barrier, inc=1, device_id={"head": lax.rem(my_head + k, PEERS)}, device_id_type=MESH
        )

    for copy in small:
        copy.wait()
    opens = flags(starts_ref)
    running = jnp.float32(1.0)
    for c in range(TILES):
        flag = opens(me * TILES + c, B)
        running = running * flag
        kc_sm[c] = flag
        mp_sm[c] = running
    running = jnp.float32(1.0)
    for c in reversed(range(TILES)):
        reach_ref[c : c + 1, :] = jnp.full((1, B), running, F32)
        running = running * kc_sm[c]

    def shard_flag(i):
        keep_sm[i] = opens(i, ROWS)

    loop(SHARDS, shard_flag)

    row = lax.broadcasted_iota(jnp.int32, (B, B), 0)
    col = lax.broadcasted_iota(jnp.int32, (B, B), 1)

    def lower(x):
        return jnp.where(row >= col, x, 0.0).astype(BF16)

    def upper(x):
        return jnp.where(row <= col, x, 0.0).astype(BF16)

    def unpack(raw, out, c):
        out[:, c] = jnp.swapaxes(raw[pl.ds(pl.multiple_of(c * B, B), B)], 0, 1)

    def states(g):
        heads = range(g * G, (g + 1) * G)

        def body(i):
            for h in heads:
                total = st[h].reshape(B, B)
                for n in range(STEP):
                    c = i * STEP + n
                    kept = kc_sm[c] * total
                    lbuf[h, c] = kept
                    total = tn(kh[h, c], vh[h, c]) + kept
                st[h] = total.reshape(SHARDS, PIECE, B)

        loop(TILES // STEP, body)

    def group(g):
        return pl.ds(g * G, G)

    def scatter(src, dst, ssem, rsem, g):
        for o in OFFSETS:
            p = at_offset(o)
            pltpu.make_async_remote_copy(
                src.at[group(g), p], dst.at[me, group(g)], ssem.at[0], rsem.at[g],
                device_id={"ctx": p}, device_id_type=MESH,
            ).start()
        dst[me, group(g)] = src[group(g), me]

    def chain(rx, px, inc, r_in, s_out, r_out, g, forward):
        arrived(rx, r_in, g)
        first = 0 if forward else SHARDS - 1
        px[first, group(g)] = jnp.zeros((G, PIECE, B), F32)

        def step(turn, total):
            i = turn if forward else SHARDS - 1 - turn
            total = rx[i, group(g)] + keep_sm[i] * total

            @pl.when(turn < SHARDS - 1)
            def _():
                px[i + 1 if forward else i - 1, group(g)] = total

            @pl.when(i != me)
            def _():
                pltpu.make_async_remote_copy(
                    px.at[i, group(g)], inc.at[me, group(g)], s_out.at[0], r_out.at[g],
                    device_id={"ctx": i}, device_id_type=MESH,
                ).start()

            return total

        lax.fori_loop(0, SHARDS, step, jnp.zeros((G, PIECE, B), F32))
        inc[me, group(g)] = px[me, group(g)]

    def arrived(dst, rsem, g):
        part = dst.at[pl.ds(0, SHARDS - 1), group(g)]
        pltpu.make_async_copy(part, part, rsem.at[g]).wait()

    def sent(buffer, ssem):
        part = buffer.at[pl.ds(0, SHARDS - 1)]
        pltpu.make_async_copy(part, part, ssem.at[0]).wait()

    st[...] = jnp.zeros_like(st)

    def unpack_half(raw, out, half):
        def body(c):
            unpack(raw, out, half * (TILES // 2) + c)

        loop(TILES // 2, body)

    for half in range(2):
        load(0, half).wait()
        unpack_half(k_raw, kh, half)
        load(1, half).wait()
        unpack_half(v_raw, vh, half)

    states(0)
    pl.semaphore_wait(barrier, SHARDS - 1 + PEERS - 1)
    scatter(st, rx, s1, r1, 0)
    for g in range(1, GROUPS):
        states(g)
        scatter(st, rx, s1, r1, g)

    for half in range(2):
        load(2, half).wait()
        unpack_half(q_raw, qh, half)
        load(3, half).wait()
        unpack_half(u_raw, uh, half)

    def scores(g):
        def body(i):
            for n in range(STEP):
                c = i * STEP + n
                for h in range(g * G, (g + 1) * G):
                    a = lower(nt(qh[h, c], kh[h, c]))
                    ah[h, c] = a
                    ath[h, c] = turn(a)

        loop(TILES // STEP, body)

    scores(0)
    for g in range(GROUPS):
        chain(rx, px, inc, r1, s2, r2, g, True)
        if g + 1 < GROUPS:
            scores(g + 1)

    for g in range(GROUPS):
        arrived(inc, r2, g)

        def body(i, g=g):
            for n in range(STEP):
                c = i * STEP + n
                sq = jnp.zeros((B, B), F32) if g == 0 else sqa[c]
                cr = jnp.zeros((B, B), F32) if g == 0 else cra[c]
                reach = mp_sm[c]
                for h in range(g * G, (g + 1) * G):
                    entry = (lbuf[h, c] + reach * inc[:, h].reshape(B, B)).astype(BF16)
                    rbuf[h, c] = entry
                    out = nn(
                        jnp.concatenate([ah[h, c], qh[h, c]], axis=1),
                        jnp.concatenate([vh[h, c], entry], axis=0),
                    )
                    att[h, c] = out
                    sq = sq + out * out
                    cr = cr + uh[h, c].astype(F32) * gain_ref[h : h + 1, :] * out
                sqa[c] = sq
                cra[c] = cr

        loop(TILES // STEP, body)

    sq_cols = jnp.zeros((B, B), F32)
    cr_cols = jnp.zeros((B, B), F32)
    for c in range(TILES):
        sq_cols = jnp.where(col == c, jnp.sum(sqa[c], axis=1, keepdims=True), sq_cols)
        cr_cols = jnp.where(col == c, jnp.sum(cra[c], axis=1, keepdims=True), cr_cols)
    stat_tx[0] = jnp.transpose(sq_cols)[:TILES]
    stat_tx[1] = jnp.transpose(cr_cols)[:TILES]

    for k in range(1, PEERS):
        pltpu.make_async_remote_copy(
            stat_tx, stat_rx.at[my_head], hs.at[0], hr.at[0],
            device_id={"head": lax.rem(my_head + k, PEERS)}, device_id_type=MESH,
        ).start()
    stat_rx[my_head] = stat_tx[...]
    others = stat_rx.at[pl.ds(0, PEERS - 1)]
    pltpu.make_async_copy(others, others, hr.at[0]).wait()
    sums = stat_rx[0]
    for k in range(1, PEERS):
        sums = sums + stat_rx[k]
    features = HEADS * HEAD_DIM
    inverse = 1.0 / jnp.sqrt(sums[0] / features + EPSILON)
    pull = inverse * inverse * inverse * sums[1] / features
    inv_cols = jnp.transpose(jnp.concatenate([inverse] * (B // TILES), axis=0))
    pull_cols = jnp.transpose(jnp.concatenate([pull] * (B // TILES), axis=0))
    for c in range(TILES):
        invb[c] = jnp.broadcast_to(inv_cols[:, c : c + 1], (B, B))
        cob[c] = jnp.broadcast_to(pull_cols[:, c : c + 1], (B, B))

    gpart[...] = jnp.zeros_like(gpart)
    st2[...] = jnp.zeros_like(st2)
    for g in range(GROUPS):

        def body(i, g=g):
            for h in range(g * G, (g + 1) * G):
                gain = gain_ref[h : h + 1, :]
                later = st2[h].reshape(B, B)
                gains = gpart[h]
                for n in range(STEP):
                    c = TILES - 1 - (i * STEP + n)
                    inv = invb[c]
                    out = att[h, c]
                    up = uh[h, c].astype(F32)
                    scaled = out * inv
                    ah[h, c] = (scaled * gain).astype(BF16)
                    grad = (inv * (up * gain) - out * cob[c]).astype(BF16)
                    gh[h, c] = grad
                    gains = gains + jnp.sum((up * scaled).reshape(B // 8, 8, B), axis=0)
                    lbuf[h, c] = later
                    later = kc_sm[c] * (tn(qh[h, c], grad) + later)
                gpart[h] = gains
                st2[h] = later.reshape(SHARDS, PIECE, B)

        loop(TILES // STEP, body)
        scatter(st2, rx2, s3, r3, g)

    for h in range(LOCAL):
        gain_tx[h : h + 1, :] = jnp.sum(gpart[h], axis=0, keepdims=True)

    for k in range(1, SHARDS):
        pltpu.make_async_remote_copy(
            gain_tx, gain_rx.at[me], gs.at[0], gr_sem.at[0],
            device_id={"ctx": lax.rem(me + k, SHARDS)}, device_id_type=MESH,
        ).start()
    gain_rx[me] = gain_tx[...]

    def pack(value, out, c):
        out[pl.ds(pl.multiple_of(c * B, B), B)] = jnp.swapaxes(value, 0, 1)

    def grad_q(g):
        def body(i):
            for n in range(STEP):
                c = i * STEP + n
                for h in range(g * G, (g + 1) * G):
                    grad = gh[h, c]
                    both = nt(grad, jnp.concatenate([vh[h, c], rbuf[h, c]], axis=0))
                    b = lower(both[:, :B])
                    bth[h, c] = turn(b)
                    rbuf[h, c] = (nn(b, kh[h, c]) + both[:, B:]).astype(BF16)

        loop(TILES // STEP, body)

    def put_normed(c):
        pack(ah[:, c], n_tok, c)

    loop(TILES, put_normed)
    for g in range(GROUPS):
        grad_q(g)
        chain(rx2, px2, inc2, r3, s4, r4, g, False)

    def put_dq(c):
        pack(rbuf[:, c], dq_tok, c)

    loop(TILES, put_dq)

    others = gain_rx.at[pl.ds(0, SHARDS - 1)]
    pltpu.make_async_copy(others, others, gr_sem.at[0]).wait()
    total = gain_rx[0]
    for k in range(1, SHARDS):
        total = total + gain_rx[k]
    dgain_ref[...] = total / math.sqrt(TOKENS)

    sent(rx, s1)
    sent(rx, s2)
    sent(rx, s3)
    sent(rx, s4)
    others = stat_rx.at[pl.ds(0, PEERS - 1)]
    pltpu.make_async_copy(others, others, hs.at[0]).wait()
    others = gain_rx.at[pl.ds(0, SHARDS - 1)]
    pltpu.make_async_copy(others, others, gs.at[0]).wait()
    for g in range(GROUPS):
        arrived(inc2, r4, g)


def finish(
    n_tok, dq_tok, qh, kh, vh, gh, ath, bth, lbuf, inc2, reach_ref, gain_sum,
    n_out, dq_out, dk_out, dv_out, gain_out,
    dk_tok, dv_tok, dkh, dvh, out_sem,
):
    whole = [
        pltpu.make_async_copy(n_tok, n_out, out_sem.at[0, 0]),
        pltpu.make_async_copy(dq_tok, dq_out, out_sem.at[1, 0]),
    ]
    for copy in whole:
        copy.start()
    def body(i):
        for n in range(PAIR):
            c = i * PAIR + n
            reach = reach_ref[pl.ds(c, 1), :]
            for h in range(LOCAL):
                leave = (lbuf[h, c] + reach * inc2[:, h].reshape(B, B)).astype(BF16)
                dk = nn(
                    jnp.concatenate([bth[h, c], vh[h, c]], axis=1),
                    jnp.concatenate([qh[h, c], turn(leave)], axis=0),
                )
                dv = nn(
                    jnp.concatenate([ath[h, c], kh[h, c]], axis=1),
                    jnp.concatenate([gh[h, c], leave], axis=0),
                )
                dkh[h, n] = dk.astype(BF16)
                dvh[h, n] = dv.astype(BF16)
        for n in range(PAIR):
            rows = pl.ds(pl.multiple_of((i * PAIR + n) * B, B), B)
            dk_tok[rows] = jnp.swapaxes(dkh[:, n], 0, 1)
            dv_tok[rows] = jnp.swapaxes(dvh[:, n], 0, 1)
        chunk_start(i)

    def chunk(stage, out, a, i):
        rows = pl.ds(i * PAIR * B, PAIR * B)
        return pltpu.make_async_copy(stage.at[rows], out.at[rows], out_sem.at[a, 1 + i])

    def chunk_start(i):
        chunk(dk_tok, dk_out, 0, i).start()
        chunk(dv_tok, dv_out, 1, i).start()

    loop(TILES // PAIR, body)
    gain_out[...] = gain_sum[...]
    for copy in whole:
        copy.wait()
    for i in range(TILES // PAIR):
        chunk(dk_tok, dk_out, 0, i).wait()
        chunk(dv_tok, dv_out, 1, i).wait()


def local(queries, key_rows, value_rows, grad_normed, norm_gain, document_starts):
    vmem = pl.BlockSpec(memory_space=pltpu.VMEM)
    tiles = (LOCAL, TILES, B, B)
    rows = (ROWS, LOCAL, HEAD_DIM)
    raw = pltpu.VMEM(rows, BF16)
    narrow = pltpu.VMEM(tiles, BF16)
    wide = pltpu.VMEM(tiles, F32)
    stats = pltpu.VMEM((TILES, B, B), F32)
    state = pltpu.VMEM((LOCAL, SHARDS, PIECE, B), F32)
    pieces = pltpu.VMEM((SHARDS, LOCAL, PIECE, B), F32)
    row = pltpu.VMEM((8, B), F32)
    hbm = pl.BlockSpec(memory_space=pltpu.HBM)
    dma = pltpu.SemaphoreType.DMA
    big = jax.ShapeDtypeStruct(rows, BF16)
    middle = pl.pallas_call(
        kernel,
        out_shape=(raw, raw, narrow, narrow, narrow, narrow, narrow, narrow, wide, pieces, row, row),
        in_specs=[hbm] * 6,
        out_specs=(vmem,) * 12,
        scratch_shapes=[row, pltpu.SMEM((6,), jnp.int32)]
        + [raw] * 4
        + [narrow, narrow, wide, narrow]
        + [stats] * 4
        + [pltpu.VMEM((LOCAL, 8, B), F32)]
        + [state, pieces, pieces, pieces, state, pieces, pieces]
        + [
            pltpu.VMEM((PEERS, 2, TILES, B), F32),
            pltpu.VMEM((2, TILES, B), F32),
            pltpu.VMEM((SHARDS, LOCAL, B), F32),
            pltpu.VMEM((LOCAL, B), F32),
        ]
        + [pltpu.SMEM((TILES,), F32)] * 2
        + [pltpu.SMEM((SHARDS,), F32)]
        + [dma((2,)), dma((4, 2))]
        + [dma((1,)), dma((GROUPS,))] * 4
        + [dma((1,))] * 4,
        compiler_params=pltpu.CompilerParams(
            collective_id=0, has_side_effects=True, vmem_limit_bytes=LIMIT
        ),
    )(queries, key_rows, value_rows, grad_normed, norm_gain, document_starts)
    pair = pltpu.VMEM((LOCAL, PAIR, B, B), BF16)
    grads = pl.pallas_call(
        finish,
        out_shape=(big,) * 4 + (jax.ShapeDtypeStruct((LOCAL, HEAD_DIM), F32),),
        in_specs=[vmem] * 12,
        out_specs=(hbm,) * 4 + (vmem,),
        scratch_shapes=[raw, raw, pair, pair]
        + [dma((2, 1 + TILES // PAIR))],
        compiler_params=pltpu.CompilerParams(vmem_limit_bytes=LIMIT2),
    )(*middle)
    return tuple(grads)


def solution(mesh):
    rows = P("ctx", "head", None)
    return jax.shard_map(
        local,
        mesh=mesh,
        in_specs=(rows, rows, rows, rows, P("head", None), P()),
        out_specs=(rows, rows, rows, rows, P("head", None)),
        check_vma=False,
    )
```

```python
import functools
import math

import jax
import jax.numpy as jnp
from jax import lax
from jax.experimental import pallas as pl
from jax.experimental.pallas import tpu as pltpu
from jax.sharding import PartitionSpec as P

HEADS = 64
HEAD_DIM = 128
EPSILON = 1e-06
TOKENS = 16384
SHARDS = 16
PEERS = 8
ROWS = 1024
LOCAL = 8
B = 128
TILES = ROWS // B
HALF = ROWS // 2
STEP = 8
PAIR = 2
LIMIT = 32 << 20
LIMIT2 = 12 << 20
GROUPS = 4
G = LOCAL // GROUPS
PIECE = HEAD_DIM // SHARDS
MESH = pl.DeviceIdType.MESH
F32 = jnp.float32
BF16 = jnp.bfloat16

OFFSETS = sorted(
    range(1, SHARDS), key=lambda o: -(min(o // 4, 4 - o // 4) + min(o % 4, 4 - o % 4))
)


def nn(a, b):
    return lax.dot_general(a, b, (((1,), (0,)), ((), ())), preferred_element_type=F32)


def nt(a, b):
    return lax.dot_general(a, b, (((1,), (1,)), ((), ())), preferred_element_type=F32)


def tn(a, b):
    return lax.dot_general(a, b, (((0,), (0,)), ((), ())), preferred_element_type=F32)


def turn(a):
    return jnp.transpose(a)


def loop(count, body):
    def step(i, carry):
        body(i)
        return carry

    lax.fori_loop(0, count, step, 0)


def flags(starts_ref):
    def opens(position, width):
        found = jnp.int32(0)
        for d in range(starts_ref.shape[0]):
            found = found + (starts_ref[d] // width == position).astype(jnp.int32)
        return 1.0 - jnp.minimum(found, 1).astype(F32)

    return opens


def kernel(
    q_hbm, k_hbm, v_hbm, u_hbm, gain_hbm, starts_hbm,
    n_tok, dq_tok, qh, kh, vh, gh, ath, bth, lbuf, inc2, dkh, dvh, reach_ref, dgain_ref,
    gain_ref, starts_ref, q_raw, k_raw, v_raw, u_raw,
    uh, ah, att, rbuf,
    sqa, cra, invb, cob, gpart,
    st, rx, px, inc, st2, rx2, px2,
    stat_rx, stat_tx, gain_rx, gain_tx,
    kc_sm, mp_sm, keep_sm,
    small_sem, in_sem, s1, r1, s2, r2, s3, r3, s4, r4, hs, hr, gs, gr_sem,
):
    me = lax.axis_index("ctx")
    my_head = lax.axis_index("head")
    y, z = me // 4, lax.rem(me, 4)

    def at_offset(o):
        return lax.rem(y + o // 4, 4) * 4 + lax.rem(z + o % 4, 4)

    hbm_in = (k_hbm, v_hbm, q_hbm, u_hbm)
    raw_in = (k_raw, v_raw, q_raw, u_raw)

    def load(a, c):
        rows = pl.ds(c * HALF, HALF)
        return pltpu.make_async_copy(hbm_in[a].at[rows], raw_in[a].at[rows], in_sem.at[a, c])

    small = [
        pltpu.make_async_copy(starts_hbm, starts_ref, small_sem.at[0]),
        pltpu.make_async_copy(gain_hbm, gain_ref, small_sem.at[1]),
    ]
    for copy in small:
        copy.start()
    for a, b in ((0, 1), (2, 3)):
        for c in range(2):
            load(a, c).start()
            load(b, c).start()

    barrier = pltpu.get_barrier_semaphore()
    for k in range(1, SHARDS):
        pl.semaphore_signal(
            barrier, inc=1, device_id={"ctx": lax.rem(me + k, SHARDS)}, device_id_type=MESH
        )
    for k in range(1, PEERS):
        pl.semaphore_signal(
            barrier, inc=1, device_id={"head": lax.rem(my_head + k, PEERS)}, device_id_type=MESH
        )

    for copy in small:
        copy.wait()
    opens = flags(starts_ref)
    running = jnp.float32(1.0)
    for c in range(TILES):
        flag = opens(me * TILES + c, B)
        running = running * flag
        kc_sm[c] = flag
        mp_sm[c] = running
    running = jnp.float32(1.0)
    for c in reversed(range(TILES)):
        reach_ref[c : c + 1, :] = jnp.full((1, B), running, F32)
        running = running * kc_sm[c]

    def shard_flag(i):
        keep_sm[i] = opens(i, ROWS)

    loop(SHARDS, shard_flag)

    row = lax.broadcasted_iota(jnp.int32, (B, B), 0)
    col = lax.broadcasted_iota(jnp.int32, (B, B), 1)

    def lower(x):
        return jnp.where(row >= col, x, 0.0).astype(BF16)

    def upper(x):
        return jnp.where(row <= col, x, 0.0).astype(BF16)

    def unpack(raw, out, c):
        out[:, c] = jnp.swapaxes(raw[pl.ds(pl.multiple_of(c * B, B), B)], 0, 1)

    def states(g):
        heads = range(g * G, (g + 1) * G)

        def body(i):
            for h in heads:
                total = st[h].reshape(B, B)
                for n in range(STEP):
                    c = i * STEP + n
                    kept = kc_sm[c] * total
                    lbuf[h, c] = kept
                    total = tn(kh[h, c], vh[h, c]) + kept
                st[h] = total.reshape(SHARDS, PIECE, B)

        loop(TILES // STEP, body)

    def group(g):
        return pl.ds(g * G, G)

    def scatter(src, dst, ssem, rsem, g):
        for o in OFFSETS:
            p = at_offset(o)
            pltpu.make_async_remote_copy(
                src.at[group(g), p], dst.at[me, group(g)], ssem.at[0], rsem.at[g],
                device_id={"ctx": p}, device_id_type=MESH,
            ).start()
        dst[me, group(g)] = src[group(g), me]

    def chain(rx, px, inc, r_in, s_out, r_out, g, forward):
        arrived(rx, r_in, g)
        order = list(range(SHARDS)) if forward else list(reversed(range(SHARDS)))
        total = jnp.zeros((G, PIECE, B), F32)
        for i in order:
            px[i, group(g)] = total
            total = rx[i, group(g)] + keep_sm[i] * total
        for o in OFFSETS:
            i = at_offset(o)
            pltpu.make_async_remote_copy(
                px.at[i, group(g)], inc.at[me, group(g)], s_out.at[0], r_out.at[g],
                device_id={"ctx": i}, device_id_type=MESH,
            ).start()
        inc[me, group(g)] = px[me, group(g)]

    def arrived(dst, rsem, g):
        part = dst.at[pl.ds(0, SHARDS - 1), group(g)]
        pltpu.make_async_copy(part, part, rsem.at[g]).wait()

    def sent(buffer, ssem):
        part = buffer.at[pl.ds(0, SHARDS - 1)]
        pltpu.make_async_copy(part, part, ssem.at[0]).wait()

    st[...] = jnp.zeros_like(st)

    def unpack_half(raw, out, half):
        def body(c):
            unpack(raw, out, half * (TILES // 2) + c)

        loop(TILES // 2, body)

    for half in range(2):
        load(0, half).wait()
        unpack_half(k_raw, kh, half)
        load(1, half).wait()
        unpack_half(v_raw, vh, half)

    states(0)
    pl.semaphore_wait(barrier, SHARDS - 1 + PEERS - 1)
    scatter(st, rx, s1, r1, 0)
    for g in range(1, GROUPS):
        states(g)
        scatter(st, rx, s1, r1, g)

    for half in range(2):
        load(2, half).wait()
        unpack_half(q_raw, qh, half)
        load(3, half).wait()
        unpack_half(u_raw, uh, half)

    def scores(g):
        def body(i):
            for n in range(STEP):
                c = i * STEP + n
                for h in range(g * G, (g + 1) * G):
                    a = lower(nt(qh[h, c], kh[h, c]))
                    ah[h, c] = a
                    ath[h, c] = turn(a)

        loop(TILES // STEP, body)

    scores(0)
    for g in range(GROUPS):
        chain(rx, px, inc, r1, s2, r2, g, True)
        if g + 1 < GROUPS:
            scores(g + 1)

    for g in range(GROUPS):
        arrived(inc, r2, g)

        def body(i, g=g):
            for n in range(STEP):
                c = i * STEP + n
                sq = jnp.zeros((B, B), F32) if g == 0 else sqa[c]
                cr = jnp.zeros((B, B), F32) if g == 0 else cra[c]
                reach = mp_sm[c]
                for h in range(g * G, (g + 1) * G):
                    entry = (lbuf[h, c] + reach * inc[:, h].reshape(B, B)).astype(BF16)
                    rbuf[h, c] = entry
                    out = nn(
                        jnp.concatenate([ah[h, c], qh[h, c]], axis=1),
                        jnp.concatenate([vh[h, c], entry], axis=0),
                    )
                    att[h, c] = out
                    sq = sq + out * out
                    cr = cr + uh[h, c].astype(F32) * gain_ref[h : h + 1, :] * out
                sqa[c] = sq
                cra[c] = cr

        loop(TILES // STEP, body)

    sq_cols = jnp.zeros((B, B), F32)
    cr_cols = jnp.zeros((B, B), F32)
    for c in range(TILES):
        sq_cols = jnp.where(col == c, jnp.sum(sqa[c], axis=1, keepdims=True), sq_cols)
        cr_cols = jnp.where(col == c, jnp.sum(cra[c], axis=1, keepdims=True), cr_cols)
    stat_tx[0] = jnp.transpose(sq_cols)[:TILES]
    stat_tx[1] = jnp.transpose(cr_cols)[:TILES]

    for k in range(1, PEERS):
        pltpu.make_async_remote_copy(
            stat_tx, stat_rx.at[my_head], hs.at[0], hr.at[0],
            device_id={"head": lax.rem(my_head + k, PEERS)}, device_id_type=MESH,
        ).start()
    stat_rx[my_head] = stat_tx[...]
    others = stat_rx.at[pl.ds(0, PEERS - 1)]
    pltpu.make_async_copy(others, others, hr.at[0]).wait()
    sums = stat_rx[0]
    for k in range(1, PEERS):
        sums = sums + stat_rx[k]
    features = HEADS * HEAD_DIM
    inverse = 1.0 / jnp.sqrt(sums[0] / features + EPSILON)
    pull = inverse * inverse * inverse * sums[1] / features
    inv_cols = jnp.transpose(jnp.concatenate([inverse] * (B // TILES), axis=0))
    pull_cols = jnp.transpose(jnp.concatenate([pull] * (B // TILES), axis=0))
    for c in range(TILES):
        invb[c] = jnp.broadcast_to(inv_cols[:, c : c + 1], (B, B))
        cob[c] = jnp.broadcast_to(pull_cols[:, c : c + 1], (B, B))

    gpart[...] = jnp.zeros_like(gpart)
    st2[...] = jnp.zeros_like(st2)
    for g in range(GROUPS):

        def body(i, g=g):
            for h in range(g * G, (g + 1) * G):
                gain = gain_ref[h : h + 1, :]
                later = st2[h].reshape(B, B)
                gains = gpart[h]
                for n in range(STEP):
                    c = TILES - 1 - (i * STEP + n)
                    inv = invb[c]
                    out = att[h, c]
                    up = uh[h, c].astype(F32)
                    scaled = out * inv
                    ah[h, c] = (scaled * gain).astype(BF16)
                    grad = (inv * (up * gain) - out * cob[c]).astype(BF16)
                    gh[h, c] = grad
                    gains = gains + jnp.sum((up * scaled).reshape(B // 8, 8, B), axis=0)
                    lbuf[h, c] = later
                    later = kc_sm[c] * (tn(qh[h, c], grad) + later)
                gpart[h] = gains
                st2[h] = later.reshape(SHARDS, PIECE, B)

        loop(TILES // STEP, body)
        scatter(st2, rx2, s3, r3, g)

    for h in range(LOCAL):
        gain_tx[h : h + 1, :] = jnp.sum(gpart[h], axis=0, keepdims=True)

    for k in range(1, SHARDS):
        pltpu.make_async_remote_copy(
            gain_tx, gain_rx.at[me], gs.at[0], gr_sem.at[0],
            device_id={"ctx": lax.rem(me + k, SHARDS)}, device_id_type=MESH,
        ).start()
    gain_rx[me] = gain_tx[...]

    def pack(value, out, c):
        out[pl.ds(pl.multiple_of(c * B, B), B)] = jnp.swapaxes(value, 0, 1)

    def grad_scores(g):
        def body(i):
            for n in range(STEP):
                c = i * STEP + n
                for h in range(g * G, (g + 1) * G):
                    b = lower(nt(gh[h, c], vh[h, c]))
                    ah[h, c] = b
                    bth[h, c] = turn(b)

        loop(TILES // STEP, body)

    def grad_q(g):
        def body(i):
            for n in range(STEP):
                c = i * STEP + n
                for h in range(g * G, (g + 1) * G):
                    dq = nn(
                        jnp.concatenate([ah[h, c], gh[h, c]], axis=1),
                        jnp.concatenate([kh[h, c], turn(rbuf[h, c])], axis=0),
                    )
                    uh[h, c] = dq.astype(BF16)

        loop(TILES // STEP, body)

    def put_normed(c):
        pack(ah[:, c], n_tok, c)

    loop(TILES, put_normed)
    for g in range(GROUPS):
        grad_scores(g)
        if g >= 1:
            chain(rx2, px2, inc2, r3, s4, r4, g - 1, False)
    grad_q(0)
    chain(rx2, px2, inc2, r3, s4, r4, GROUPS - 1, False)
    for g in range(1, GROUPS):
        grad_q(g)

    def put_dq(c):
        pack(uh[:, c], dq_tok, c)

    loop(TILES, put_dq)

    others = gain_rx.at[pl.ds(0, SHARDS - 1)]
    pltpu.make_async_copy(others, others, gr_sem.at[0]).wait()
    total = gain_rx[0]
    for k in range(1, SHARDS):
        total = total + gain_rx[k]
    dgain_ref[...] = total / math.sqrt(TOKENS)

    for g in range(GROUPS - 1):
        arrived(inc2, r4, g)

        def body(i, g=g):
            for n in range(STEP):
                c = i * STEP + n
                for h in range(g * G, (g + 1) * G):
                    dk, dv = tail(qh, kh, vh, gh, ath, bth, lbuf, inc2, reach_ref, h, c)
                    dkh[h, c] = dk
                    dvh[h, c] = dv

        loop(TILES // STEP, body)

    sent(rx, s1)
    sent(rx, s2)
    sent(rx, s3)
    sent(rx, s4)
    others = stat_rx.at[pl.ds(0, PEERS - 1)]
    pltpu.make_async_copy(others, others, hs.at[0]).wait()
    others = gain_rx.at[pl.ds(0, SHARDS - 1)]
    pltpu.make_async_copy(others, others, gs.at[0]).wait()
    arrived(inc2, r4, GROUPS - 1)


def tail(qh, kh, vh, gh, ath, bth, lbuf, inc2, reach_ref, h, c):
    reach = reach_ref[pl.ds(c, 1), :]
    leave = (lbuf[h, c] + reach * inc2[:, h].reshape(B, B)).astype(BF16)
    dk = nn(
        jnp.concatenate([bth[h, c], vh[h, c]], axis=1),
        jnp.concatenate([qh[h, c], turn(leave)], axis=0),
    )
    dv = nn(
        jnp.concatenate([ath[h, c], kh[h, c]], axis=1),
        jnp.concatenate([gh[h, c], leave], axis=0),
    )
    return dk.astype(BF16), dv.astype(BF16)


def finish(
    n_tok, dq_tok, qh, kh, vh, gh, ath, bth, lbuf, inc2, dkh, dvh, reach_ref, gain_sum,
    n_out, dq_out, dk_out, dv_out, gain_out,
    dk_tok, dv_tok, dk_last, dv_last, out_sem,
):
    whole = [
        pltpu.make_async_copy(n_tok, n_out, out_sem.at[0, 0]),
        pltpu.make_async_copy(dq_tok, dq_out, out_sem.at[1, 0]),
    ]
    for copy in whole:
        copy.start()
    first = LOCAL - G
    for c in range(TILES):
        for h in range(G):
            dk, dv = tail(
                qh, kh, vh, gh, ath, bth, lbuf, inc2, reach_ref, first + h, c
            )
            dk_last[h, c] = dk
            dv_last[h, c] = dv

    def pack(head, last, out, c):
        rows = pl.ds(pl.multiple_of(c * B, B), B)
        whole = jnp.concatenate([head[:first, c], last[:, c]], axis=0)
        out[rows] = jnp.swapaxes(whole, 0, 1)

    def body(i):
        for n in range(PAIR):
            pack(dkh, dk_last, dk_tok, i * PAIR + n)
            pack(dvh, dv_last, dv_tok, i * PAIR + n)
        chunk_start(i)

    def chunk(stage, out, a, i):
        rows = pl.ds(i * PAIR * B, PAIR * B)
        return pltpu.make_async_copy(stage.at[rows], out.at[rows], out_sem.at[a, 1 + i])

    def chunk_start(i):
        chunk(dk_tok, dk_out, 0, i).start()
        chunk(dv_tok, dv_out, 1, i).start()

    loop(TILES // PAIR, body)
    gain_out[...] = gain_sum[...]
    for copy in whole:
        copy.wait()
    for i in range(TILES // PAIR):
        chunk(dk_tok, dk_out, 0, i).wait()
        chunk(dv_tok, dv_out, 1, i).wait()


def local(queries, key_rows, value_rows, grad_normed, norm_gain, document_starts):
    vmem = pl.BlockSpec(memory_space=pltpu.VMEM)
    tiles = (LOCAL, TILES, B, B)
    rows = (ROWS, LOCAL, HEAD_DIM)
    raw = pltpu.VMEM(rows, BF16)
    narrow = pltpu.VMEM(tiles, BF16)
    wide = pltpu.VMEM(tiles, F32)
    stats = pltpu.VMEM((TILES, B, B), F32)
    state = pltpu.VMEM((LOCAL, SHARDS, PIECE, B), F32)
    pieces = pltpu.VMEM((SHARDS, LOCAL, PIECE, B), F32)
    row = pltpu.VMEM((8, B), F32)
    hbm = pl.BlockSpec(memory_space=pltpu.HBM)
    dma = pltpu.SemaphoreType.DMA
    big = jax.ShapeDtypeStruct(rows, BF16)
    middle = pl.pallas_call(
        kernel,
        out_shape=(raw, raw, narrow, narrow, narrow, narrow, narrow, narrow, wide, pieces)
        + (narrow, narrow, row, row),
        in_specs=[hbm] * 6,
        out_specs=(vmem,) * 14,
        scratch_shapes=[row, pltpu.SMEM((6,), jnp.int32)]
        + [raw] * 4
        + [narrow, narrow, wide, narrow]
        + [stats] * 4
        + [pltpu.VMEM((LOCAL, 8, B), F32)]
        + [state, pieces, pieces, pieces, state, pieces, pieces]
        + [
            pltpu.VMEM((PEERS, 2, TILES, B), F32),
            pltpu.VMEM((2, TILES, B), F32),
            pltpu.VMEM((SHARDS, LOCAL, B), F32),
            pltpu.VMEM((LOCAL, B), F32),
        ]
        + [pltpu.SMEM((TILES,), F32)] * 2
        + [pltpu.SMEM((SHARDS,), F32)]
        + [dma((2,)), dma((4, 2))]
        + [dma((1,)), dma((GROUPS,))] * 4
        + [dma((1,))] * 4,
        compiler_params=pltpu.CompilerParams(
            collective_id=0, has_side_effects=True, vmem_limit_bytes=LIMIT
        ),
    )(queries, key_rows, value_rows, grad_normed, *(pltpu.with_memory_space_constraint(a, pltpu.HBM) for a in (norm_gain, document_starts)))
    pair = pltpu.VMEM((G, TILES, B, B), BF16)
    grads = pl.pallas_call(
        finish,
        out_shape=(big,) * 4 + (jax.ShapeDtypeStruct((LOCAL, HEAD_DIM), F32),),
        in_specs=[vmem] * 14,
        out_specs=(hbm,) * 4 + (vmem,),
        scratch_shapes=[raw, raw, pair, pair]
        + [dma((2, 1 + TILES // PAIR))],
        compiler_params=pltpu.CompilerParams(vmem_limit_bytes=LIMIT2),
    )(*middle)
    return tuple(grads)


def solution(mesh):
    rows = P("ctx", "head", None)
    return jax.shard_map(
        local,
        mesh=mesh,
        in_specs=(rows, rows, rows, rows, P("head", None), P()),
        out_specs=(rows, rows, rows, rows, P("head", None)),
        check_vma=False,
    )
```

```python
import functools
import math

import jax
import jax.numpy as jnp
from jax import lax
from jax.experimental import pallas as pl
from jax.experimental.pallas import tpu as pltpu
from jax.sharding import PartitionSpec as P

HEADS = 64
HEAD_DIM = 128
EPSILON = 1e-06
TOKENS = 16384
SHARDS = 16
PEERS = 8
ROWS = 1024
LOCAL = 8
B = 128
TILES = ROWS // B
HALF = ROWS // 2
STEP = 8
PAIR = 2
ROWS_STEP = 32
LIMIT = 32 << 20
LIMIT2 = 12 << 20
GROUPS = 4
G = LOCAL // GROUPS
PIECE = HEAD_DIM // SHARDS
MESH = pl.DeviceIdType.MESH
F32 = jnp.float32
BF16 = jnp.bfloat16

OFFSETS = sorted(
    range(1, SHARDS), key=lambda o: -(min(o // 4, 4 - o // 4) + min(o % 4, 4 - o % 4))
)


def nn(a, b):
    return lax.dot_general(a, b, (((1,), (0,)), ((), ())), preferred_element_type=F32)


def nt(a, b):
    return lax.dot_general(a, b, (((1,), (1,)), ((), ())), preferred_element_type=F32)


def tn(a, b):
    return lax.dot_general(a, b, (((0,), (0,)), ((), ())), preferred_element_type=F32)


def turn(a):
    return jnp.transpose(a)


def loop(count, body):
    if count == 1:
        return body(0)

    def step(i, carry):
        body(i)
        return carry

    lax.fori_loop(0, count, step, 0)


def flags(starts_ref):
    def opens(position, width):
        found = jnp.int32(0)
        for d in range(starts_ref.shape[0]):
            found = found + (starts_ref[d] // width == position).astype(jnp.int32)
        return 1.0 - jnp.minimum(found, 1).astype(F32)

    return opens


def kernel(
    q_hbm, k_hbm, v_hbm, u_hbm, gain_hbm, starts_hbm,
    n_tok, dq_tok, qh, kh, vh, gh, ath, bth, lbuf, inc2, dkh, dvh, reach_ref, dgain_ref,
    gain_ref, starts_ref, q_raw, k_raw, v_raw, u_raw,
    uh, ah, att, rbuf,
    sqa, cra, invb, cob, gpart,
    st, rx, px, inc, st2, rx2, px2,
    stat_rx, stat_tx, gain_rx, gain_tx, gain_sum, gain_all,
    kc_sm, mp_sm, keep_sm,
    small_sem, in_sem, s1, r1, s2, r2, s3, r3, s4, r4, hs, hr, gs, gr_sem,
):
    me = lax.axis_index("ctx")
    my_head = lax.axis_index("head")
    y, z = me // 4, lax.rem(me, 4)

    def at_offset(o):
        return lax.rem(y + o // 4, 4) * 4 + lax.rem(z + o % 4, 4)

    barrier = pltpu.get_barrier_semaphore()
    for o in OFFSETS:
        pl.semaphore_signal(
            barrier, inc=1, device_id={"ctx": at_offset(o)}, device_id_type=MESH
        )
    for k in range(1, PEERS):
        pl.semaphore_signal(
            barrier, inc=1, device_id={"head": lax.rem(my_head + k, PEERS)}, device_id_type=MESH
        )

    hbm_in = (k_hbm, v_hbm, q_hbm, u_hbm)
    raw_in = (k_raw, v_raw, q_raw, u_raw)

    def load(a, c):
        rows = pl.ds(c * HALF, HALF)
        return pltpu.make_async_copy(hbm_in[a].at[rows], raw_in[a].at[rows], in_sem.at[a, c])

    small = [
        pltpu.make_async_copy(starts_hbm, starts_ref, small_sem.at[0]),
        pltpu.make_async_copy(gain_hbm, gain_ref, small_sem.at[1]),
    ]
    for copy in small:
        copy.start()
    for a, b in ((0, 1), (2, 3)):
        for c in range(2):
            load(a, c).start()
            load(b, c).start()

    for copy in small:
        copy.wait()
    opens = flags(starts_ref)
    running = jnp.float32(1.0)
    for c in range(TILES):
        flag = opens(me * TILES + c, B)
        running = running * flag
        kc_sm[c] = flag
        mp_sm[c] = running
    running = jnp.float32(1.0)
    for c in reversed(range(TILES)):
        reach_ref[c : c + 1, :] = jnp.full((1, B), running, F32)
        running = running * kc_sm[c]

    def shard_flag(i):
        keep_sm[i] = opens(i, ROWS)

    loop(SHARDS, shard_flag)

    row = lax.broadcasted_iota(jnp.int32, (B, B), 0)
    col = lax.broadcasted_iota(jnp.int32, (B, B), 1)

    def lower(x):
        return jnp.where(row >= col, x, 0.0).astype(BF16)

    def upper(x):
        return jnp.where(row <= col, x, 0.0).astype(BF16)

    def unpack(raw, out, c):
        out[:, c] = jnp.swapaxes(raw[pl.ds(pl.multiple_of(c * B, B), B)], 0, 1)

    def states(g):
        heads = range(g * G, (g + 1) * G)

        def body(i):
            for h in heads:
                total = st[h].reshape(B, B)
                for n in range(STEP):
                    c = i * STEP + n
                    kept = kc_sm[c] * total
                    lbuf[h, c] = kept
                    total = tn(kh[h, c], vh[h, c]) + kept
                st[h] = total.reshape(SHARDS, PIECE, B)

        loop(TILES // STEP, body)

    def group(g):
        return pl.ds(g * G, G)

    def scatter(src, dst, ssem, rsem, g):
        for o in OFFSETS:
            p = at_offset(o)
            pltpu.make_async_remote_copy(
                src.at[group(g), p], dst.at[me, group(g)], ssem.at[0], rsem.at[g],
                device_id={"ctx": p}, device_id_type=MESH,
            ).start()
        dst[me, group(g)] = src[group(g), me]

    def chain(rx, px, inc, r_in, s_out, r_out, g, forward):
        arrived(rx, r_in, g)
        order = list(range(SHARDS)) if forward else list(reversed(range(SHARDS)))
        total = jnp.zeros((G, PIECE, B), F32)
        for i in order:
            px[i, group(g)] = total
            total = rx[i, group(g)] + keep_sm[i] * total
        for o in OFFSETS:
            i = at_offset(o)
            pltpu.make_async_remote_copy(
                px.at[i, group(g)], inc.at[me, group(g)], s_out.at[0], r_out.at[g],
                device_id={"ctx": i}, device_id_type=MESH,
            ).start()
        inc[me, group(g)] = px[me, group(g)]

    def arrived(dst, rsem, g):
        part = dst.at[pl.ds(0, SHARDS - 1), group(g)]
        pltpu.make_async_copy(part, part, rsem.at[g]).wait()

    def sent(buffer, ssem):
        part = buffer.at[pl.ds(0, SHARDS - 1)]
        pltpu.make_async_copy(part, part, ssem.at[0]).wait()

    st[...] = jnp.zeros_like(st)

    def unpack_half(raw, out, half):
        def body(c):
            unpack(raw, out, half * (TILES // 2) + c)

        loop(TILES // 2, body)

    for half in range(2):
        load(0, half).wait()
        unpack_half(k_raw, kh, half)
        load(1, half).wait()
        unpack_half(v_raw, vh, half)

    for g in range(GROUPS):
        states(g)
    pl.semaphore_wait(barrier, SHARDS - 1 + PEERS - 1)
    for g in range(GROUPS):
        scatter(st, rx, s1, r1, g)

    for half in range(2):
        load(2, half).wait()
        unpack_half(q_raw, qh, half)
        load(3, half).wait()
        unpack_half(u_raw, uh, half)

    def scores(g):
        def body(i):
            for n in range(STEP):
                c = i * STEP + n
                for h in range(g * G, (g + 1) * G):
                    a = lower(nt(qh[h, c], kh[h, c]))
                    ah[h, c] = a
                    ath[h, c] = turn(a)

        loop(TILES // STEP, body)

    scores(0)
    for g in range(GROUPS):
        chain(rx, px, inc, r1, s2, r2, g, True)
        if g + 1 < GROUPS:
            scores(g + 1)

    sq_cols = jnp.zeros((B, B), F32)
    cr_cols = jnp.zeros((B, B), F32)
    for g in range(GROUPS):
        arrived(inc, r2, g)
        for c in range(TILES):
            sq = jnp.zeros((B, B), F32) if g == 0 else sqa[c]
            cr = jnp.zeros((B, B), F32) if g == 0 else cra[c]
            reach = mp_sm[c]
            for h in range(g * G, (g + 1) * G):
                entry = (lbuf[h, c] + reach * inc[:, h].reshape(B, B)).astype(BF16)
                rbuf[h, c] = entry
                out = nn(
                    jnp.concatenate([ah[h, c], qh[h, c]], axis=1),
                    jnp.concatenate([vh[h, c], entry], axis=0),
                )
                att[h, c] = out
                sq = sq + out * out
                cr = cr + uh[h, c].astype(F32) * gain_ref[h : h + 1, :] * out
            if g < GROUPS - 1:
                sqa[c] = sq
                cra[c] = cr
            else:
                sq_cols = jnp.where(col == c, jnp.sum(sq, axis=1, keepdims=True), sq_cols)
                cr_cols = jnp.where(col == c, jnp.sum(cr, axis=1, keepdims=True), cr_cols)

    stat_tx[0] = jnp.transpose(sq_cols)[:TILES]
    stat_tx[1] = jnp.transpose(cr_cols)[:TILES]

    for k in range(1, PEERS):
        pltpu.make_async_remote_copy(
            stat_tx, stat_rx.at[my_head], hs.at[0], hr.at[0],
            device_id={"head": lax.rem(my_head + k, PEERS)}, device_id_type=MESH,
        ).start()
    stat_rx[my_head] = stat_tx[...]
    others = stat_rx.at[pl.ds(0, PEERS - 1)]
    pltpu.make_async_copy(others, others, hr.at[0]).wait()
    sums = stat_rx[0]
    for k in range(1, PEERS):
        sums = sums + stat_rx[k]
    features = HEADS * HEAD_DIM
    inverse = 1.0 / jnp.sqrt(sums[0] / features + EPSILON)
    pull = inverse * inverse * inverse * sums[1] / features
    inv_cols = jnp.transpose(jnp.concatenate([inverse] * (B // TILES), axis=0))
    pull_cols = jnp.transpose(jnp.concatenate([pull] * (B // TILES), axis=0))
    for c in range(TILES):
        invb[c] = jnp.broadcast_to(inv_cols[:, c : c + 1], (B, B))
        cob[c] = jnp.broadcast_to(pull_cols[:, c : c + 1], (B, B))

    gpart[...] = jnp.zeros_like(gpart)
    st2[...] = jnp.zeros_like(st2)
    for g in range(GROUPS):

        def body(i, g=g):
            for h in range(g * G, (g + 1) * G):
                gain = gain_ref[h : h + 1, :]
                later = st2[h].reshape(B, B)
                gains = gpart[h]
                for n in range(STEP):
                    c = TILES - 1 - (i * STEP + n)
                    for r in range(0, B, ROWS_STEP):
                        part = slice(r, r + ROWS_STEP)
                        inv = invb[c, part]
                        out = att[h, c, part]
                        up = uh[h, c, part].astype(F32)
                        scaled = out * inv
                        ah[h, c, part] = (scaled * gain).astype(BF16)
                        grad = inv * (up * gain) - out * cob[c, part]
                        gh[h, c, part] = grad.astype(BF16)
                        gains = gains + jnp.sum(
                            (up * scaled).reshape(ROWS_STEP // 8, 8, B), axis=0
                        )
                    lbuf[h, c] = later
                    later = kc_sm[c] * (tn(qh[h, c], gh[h, c]) + later)
                gpart[h] = gains
                st2[h] = later.reshape(SHARDS, PIECE, B)

        loop(TILES // STEP, body)
        scatter(st2, rx2, s3, r3, g)

    for h in range(LOCAL):
        gain_tx[h] = jnp.sum(gpart[h], axis=0, keepdims=True)

        @pl.when(me != h)
        def _(h=h):
            pltpu.make_async_remote_copy(
                gain_tx.at[h], gain_rx.at[me], gs.at[0], gr_sem.at[0],
                device_id={"ctx": h}, device_id_type=MESH,
            ).start()

        @pl.when(me == h)
        def _(h=h):
            gain_rx[me] = gain_tx[h]

    def rows_wait(buffer, count, sem):
        some = buffer.at[pl.ds(0, count)]
        pltpu.make_async_copy(some, some, sem).wait()

    def gain_sums():
        @pl.when(me < LOCAL)
        def _():
            rows_wait(gain_rx, SHARDS - 1, gr_sem.at[0])
            total = gain_rx[0]
            for k in range(1, SHARDS):
                total = total + gain_rx[k]
            total = total / math.sqrt(TOKENS)
            gain_sum[...] = total
            gain_all[me] = total
            for o in OFFSETS:
                pltpu.make_async_remote_copy(
                    gain_sum, gain_all.at[me], gs.at[1], gr_sem.at[1],
                    device_id={"ctx": at_offset(o)}, device_id_type=MESH,
                ).start()

    def gain_done():
        @pl.when(me < LOCAL)
        def _():
            rows_wait(gain_all, LOCAL - 1, gr_sem.at[1])
            rows_wait(gain_all, LOCAL - 1, gs.at[0])
            rows_wait(gain_rx, SHARDS - 1, gs.at[1])

        @pl.when(me >= LOCAL)
        def _():
            rows_wait(gain_all, LOCAL, gr_sem.at[1])
            rows_wait(gain_all, LOCAL, gs.at[0])

        for h in range(LOCAL):
            dgain_ref[h : h + 1, :] = gain_all[h]

    def pack(value, out, c):
        out[pl.ds(pl.multiple_of(c * B, B), B)] = jnp.swapaxes(value, 0, 1)

    def grad_scores(g):
        def body(i):
            for n in range(STEP):
                c = i * STEP + n
                for h in range(g * G, (g + 1) * G):
                    b = lower(nt(gh[h, c], vh[h, c]))
                    ah[h, c] = b
                    bth[h, c] = turn(b)

        loop(TILES // STEP, body)

    def grad_q(g):
        def body(i):
            for n in range(STEP):
                c = i * STEP + n
                for h in range(g * G, (g + 1) * G):
                    dq = nn(
                        jnp.concatenate([ah[h, c], gh[h, c]], axis=1),
                        jnp.concatenate([kh[h, c], turn(rbuf[h, c])], axis=0),
                    )
                    uh[h, c] = dq.astype(BF16)

        loop(TILES // STEP, body)

    def put_normed(c):
        pack(ah[:, c], n_tok, c)

    loop(TILES, put_normed)
    for g in range(GROUPS):
        grad_scores(g)
        if g >= 1:
            chain(rx2, px2, inc2, r3, s4, r4, g - 1, False)
        if g == GROUPS - 1:
            gain_sums()
    for g in range(GROUPS // 2):
        grad_q(g)
    chain(rx2, px2, inc2, r3, s4, r4, GROUPS - 1, False)
    for g in range(GROUPS // 2, GROUPS):
        grad_q(g)

    def put_dq(c):
        pack(uh[:, c], dq_tok, c)

    loop(TILES, put_dq)

    for g in range(GROUPS - 1):
        arrived(inc2, r4, g)

        def body(i, g=g):
            for n in range(STEP):
                c = i * STEP + n
                for h in range(g * G, (g + 1) * G):
                    dk, dv = tail(qh, kh, vh, gh, ath, bth, lbuf, inc2, reach_ref, h, c)
                    dkh[h, c] = dk
                    dvh[h, c] = dv

        loop(TILES // STEP, body)

    sent(rx, s1)
    sent(rx, s2)
    sent(rx, s3)
    sent(rx, s4)
    others = stat_rx.at[pl.ds(0, PEERS - 1)]
    pltpu.make_async_copy(others, others, hs.at[0]).wait()
    gain_done()
    arrived(inc2, r4, GROUPS - 1)


def tail(qh, kh, vh, gh, ath, bth, lbuf, inc2, reach_ref, h, c):
    reach = reach_ref[pl.ds(c, 1), :]
    leave = (lbuf[h, c] + reach * inc2[:, h].reshape(B, B)).astype(BF16)
    dk = nn(
        jnp.concatenate([bth[h, c], vh[h, c]], axis=1),
        jnp.concatenate([qh[h, c], turn(leave)], axis=0),
    )
    dv = nn(
        jnp.concatenate([ath[h, c], kh[h, c]], axis=1),
        jnp.concatenate([gh[h, c], leave], axis=0),
    )
    return dk.astype(BF16), dv.astype(BF16)


def finish(
    n_tok, dq_tok, qh, kh, vh, gh, ath, bth, lbuf, inc2, dkh, dvh, reach_ref, gain_sum,
    n_out, dq_out, dk_out, dv_out, gain_out,
    dk_tok, dv_tok, dk_last, dv_last, out_sem,
):
    whole = [
        pltpu.make_async_copy(n_tok, n_out, out_sem.at[0, 0]),
        pltpu.make_async_copy(dq_tok, dq_out, out_sem.at[1, 0]),
    ]
    for copy in whole:
        copy.start()
    first = LOCAL - G

    def last_group(i):
        for c in range(i * PAIR, (i + 1) * PAIR):
            for h in range(G):
                dk, dv = tail(
                    qh, kh, vh, gh, ath, bth, lbuf, inc2, reach_ref, first + h, c
                )
                dk_last[h, c] = dk
                dv_last[h, c] = dv

    def pack(head, last, out, c):
        rows = pl.ds(c * B, B)
        whole = jnp.concatenate([head[:first, c], last[:, c]], axis=0)
        out[rows] = jnp.swapaxes(whole, 0, 1)

    def chunk(stage, out, a, i):
        rows = pl.ds(i * PAIR * B, PAIR * B)
        return pltpu.make_async_copy(stage.at[rows], out.at[rows], out_sem.at[a, 1 + i])

    def chunk_start(i):
        chunk(dk_tok, dk_out, 0, i).start()
        chunk(dv_tok, dv_out, 1, i).start()

    last_group(0)
    for i in range(TILES // PAIR):
        if i + 1 < TILES // PAIR:
            last_group(i + 1)
        for n in range(PAIR):
            pack(dkh, dk_last, dk_tok, i * PAIR + n)
            pack(dvh, dv_last, dv_tok, i * PAIR + n)
        chunk_start(i)
    gain_out[...] = gain_sum[...]
    for copy in whole:
        copy.wait()
    for i in range(TILES // PAIR):
        chunk(dk_tok, dk_out, 0, i).wait()
        chunk(dv_tok, dv_out, 1, i).wait()


def local(queries, key_rows, value_rows, grad_normed, norm_gain, document_starts):
    vmem = pl.BlockSpec(memory_space=pltpu.VMEM)
    tiles = (LOCAL, TILES, B, B)
    rows = (ROWS, LOCAL, HEAD_DIM)
    raw = pltpu.VMEM(rows, BF16)
    narrow = pltpu.VMEM(tiles, BF16)
    wide = pltpu.VMEM(tiles, F32)
    stats = pltpu.VMEM((TILES, B, B), F32)
    state = pltpu.VMEM((LOCAL, SHARDS, PIECE, B), F32)
    pieces = pltpu.VMEM((SHARDS, LOCAL, PIECE, B), F32)
    row = pltpu.VMEM((8, B), F32)
    hbm = pl.BlockSpec(memory_space=pltpu.HBM)
    dma = pltpu.SemaphoreType.DMA
    big = jax.ShapeDtypeStruct(rows, BF16)
    middle = pl.pallas_call(
        kernel,
        out_shape=(raw, raw, narrow, narrow, narrow, narrow, narrow, narrow, wide, pieces)
        + (narrow, narrow, row, row),
        in_specs=[hbm] * 6,
        out_specs=(vmem,) * 14,
        scratch_shapes=[row, pltpu.SMEM((6,), jnp.int32)]
        + [raw] * 4
        + [narrow, narrow, wide, narrow]
        + [stats] * 4
        + [pltpu.VMEM((LOCAL, 8, B), F32)]
        + [state, pieces, pieces, pieces, state, pieces, pieces]
        + [
            pltpu.VMEM((PEERS, 2, TILES, B), F32),
            pltpu.VMEM((2, TILES, B), F32),
            pltpu.VMEM((SHARDS, 1, B), F32),
            pltpu.VMEM((LOCAL, 1, B), F32),
            pltpu.VMEM((1, B), F32),
            pltpu.VMEM((LOCAL, 1, B), F32),
        ]
        + [pltpu.SMEM((TILES,), F32)] * 2
        + [pltpu.SMEM((SHARDS,), F32)]
        + [dma((2,)), dma((4, 2))]
        + [dma((1,)), dma((GROUPS,))] * 4
        + [dma((1,))] * 2
        + [dma((2,))] * 2,
        compiler_params=pltpu.CompilerParams(
            collective_id=0, has_side_effects=True, vmem_limit_bytes=LIMIT
        ),
    )(queries, key_rows, value_rows, grad_normed, *(pltpu.with_memory_space_constraint(a, pltpu.HBM) for a in (norm_gain, document_starts)))
    pair = pltpu.VMEM((G, TILES, B, B), BF16)
    grads = pl.pallas_call(
        finish,
        out_shape=(big,) * 4 + (jax.ShapeDtypeStruct((LOCAL, HEAD_DIM), F32),),
        in_specs=[vmem] * 14,
        out_specs=(hbm,) * 4 + (vmem,),
        scratch_shapes=[raw, raw, pair, pair]
        + [dma((2, 1 + TILES // PAIR))],
        compiler_params=pltpu.CompilerParams(vmem_limit_bytes=LIMIT2),
    )(*middle)
    return tuple(grads)


def solution(mesh):
    rows = P("ctx", "head", None)
    return jax.shard_map(
        local,
        mesh=mesh,
        in_specs=(rows, rows, rows, rows, P("head", None), P()),
        out_specs=(rows, rows, rows, rows, P("head", None)),
        check_vma=False,
    )
```
